32 devices in a mesh: seq: 16 (over z, x, core), dp: 2 (over y).
Axes of the slice: x: 2, y: 2, z: 4, core: 2. Of those that a mesh axis runs over, the one named last changes fastest.
Arguments:
- queries: bfloat16 [2, 1024, 2048], P(None, 'seq', 'dp'), may hold values from -10 to 10
- key_rows: bfloat16 [2, 1024, 2048], P(None, 'seq', 'dp'), may hold values from -10 to 10
- value_rows: bfloat16 [2, 1024, 2048], P(None, 'seq', 'dp'), may hold values from -6 to 6
- query_tangent: bfloat16 [2, 1024, 2048], P(None, 'seq', 'dp'), may hold values from -6 to 6
- key_tangent: bfloat16 [2, 1024, 2048], P(None, 'seq', 'dp'), may hold values from -6 to 6
- out_adjoint: bfloat16 [2, 1024, 2048], P(None, 'seq', 'dp'), may hold values from -6 to 6
Outputs:
- query_product: bfloat16 [2, 1024, 2048], P(None, 'seq', 'dp')
- key_product: bfloat16 [2, 1024, 2048], P(None, 'seq', 'dp')
- value_product: bfloat16 [2, 1024, 2048], P(None, 'seq', 'dp')
- curvature: float32 [2, 16], replicated
The draws below stay inside these ranges and needn't reach their ends.
All inputs are finite; a program needn't handle non-finite values.
Results may differ from the reference program's by a relative error of at most 0.0051.
Values may be sent and summed in bfloat16 or wider, within the bound.
A program may use at most 64 MiB of HBM per device.

```python
import jax
import jax.numpy as jnp
from jax import lax

HEAD_DIM = 128
SEQUENCE_TOKENS = 1024
HEADS = 16
BATCH_SEQUENCES = 2


def draw_pair(key):
    root_random_key = jax.random.fold_in(key, 7)
    random_key_for_query, random_key_for_keys = jax.random.split(root_random_key, 2)
    shape = (BATCH_SEQUENCES, SEQUENCE_TOKENS, HEADS * HEAD_DIM)
    query_draw = jax.random.normal(random_key_for_query, shape, jnp.float32)
    keys_draw = jax.random.normal(random_key_for_keys, shape, jnp.float32)
    query_draw = jnp.clip(query_draw, -10.0, 10.0)
    keys_draw = jnp.clip(keys_draw, -10.0, 10.0)
    return (query_draw, keys_draw)


def draw_queries(key, part):
    return draw_pair(key)[0].astype(jnp.bfloat16)


def draw_key_rows(key, part):
    return draw_pair(key)[1].astype(jnp.bfloat16)


def shard_levels(key, shape, pieces, least, largest):
    def one(dim, shards_of):
        draws = jax.random.uniform(jax.random.fold_in(jax.random.fold_in(key, 6), dim), (shards_of,), jnp.float32, least / len(pieces), largest / len(pieces))
        return jnp.repeat(jnp.exp(draws), shape[dim] // shards_of).reshape((-1,) + (1,) * (len(shape) - dim - 1))

    factor_of = one(*pieces[0])
    for cut in pieces[1:]:
        factor_of = factor_of * one(*cut)
    return factor_of


def normal_values(stream_key, dims, width, bound, shards=(), dtype=jnp.bfloat16):
    level = shard_levels(stream_key, dims, shards, -0.22, 0.18) if shards else 1.0
    values = jax.random.normal(stream_key, dims, jnp.float32) * width * level
    return jnp.minimum(jnp.maximum(values, -bound), bound).astype(dtype)


def setup_inputs(seed: int = 0) -> dict:
    key_list = jax.random.split(jax.random.key(seed), 7)
    queries = draw_queries(jax.random.fold_in(key_list[6], 71), 0)
    key_rows = draw_key_rows(jax.random.fold_in(key_list[6], 71), 0)
    value_rows = normal_values(key_list[2], (BATCH_SEQUENCES, SEQUENCE_TOKENS, HEADS * HEAD_DIM), 1.0, 6.0, ((1, 16), (2, 2)))
    query_tangent = normal_values(key_list[3], (BATCH_SEQUENCES, SEQUENCE_TOKENS, HEADS * HEAD_DIM), 1.0, 6.0, ((1, 16), (2, 2)))
    key_tangent = normal_values(key_list[4], (BATCH_SEQUENCES, SEQUENCE_TOKENS, HEADS * HEAD_DIM), 1.0, 6.0, ((1, 16), (2, 2)))
    out_adjoint = normal_values(key_list[5], (BATCH_SEQUENCES, SEQUENCE_TOKENS, HEADS * HEAD_DIM), 1.0, 6.0, ((1, 16), (2, 2)))
    return dict(queries=queries, key_rows=key_rows, value_rows=value_rows, query_tangent=query_tangent, key_tangent=key_tangent, out_adjoint=out_adjoint)


def head_terms(items):
    query, keyset, values_in, tquery, tkey, adjoint = items
    factor = HEAD_DIM ** -0.5
    length = query.shape[0]
    position = jnp.arange(length)
    causal = position[:, None] >= position[None, :]
    scores = factor * jnp.dot(query, keyset.T, preferred_element_type=jnp.float32)
    scores = jnp.where(causal, scores, -jnp.inf)
    top_score = jnp.max(scores, axis=1, keepdims=True)
    weights = jnp.exp(scores - top_score)
    probs = weights / jnp.sum(weights, axis=1, keepdims=True)
    tangent_scores = factor * (jnp.dot(tquery, keyset.T, preferred_element_type=jnp.float32) + jnp.dot(query, tkey.T, preferred_element_type=jnp.float32))
    mean_tangent = jnp.sum(probs * tangent_scores, axis=1, keepdims=True)
    tangent_probs = probs * (tangent_scores - mean_tangent)
    grad_probs = jnp.dot(adjoint, values_in.T, preferred_element_type=jnp.float32)
    delta = jnp.sum(probs * grad_probs, axis=1, keepdims=True)
    grad_scores = probs * (grad_probs - delta)
    tangent_delta = jnp.sum(tangent_probs * grad_probs, axis=1, keepdims=True)
    second_scores = tangent_probs * (grad_probs - delta) - probs * tangent_delta
    tprob_low = tangent_probs.astype(jnp.bfloat16)
    gscore_low = grad_scores.astype(jnp.bfloat16)
    second_low = second_scores.astype(jnp.bfloat16)
    value_hvp = jnp.dot(tprob_low.T, adjoint, preferred_element_type=jnp.float32)
    query_hvp = factor * (jnp.dot(second_low, keyset, preferred_element_type=jnp.float32) + jnp.dot(gscore_low, tkey, preferred_element_type=jnp.float32))
    key_hvp = factor * (jnp.dot(second_low.T, query, preferred_element_type=jnp.float32) + jnp.dot(gscore_low.T, tquery, preferred_element_type=jnp.float32))
    kappa = jnp.sum(tquery.astype(jnp.float32) * query_hvp) + jnp.sum(tkey.astype(jnp.float32) * key_hvp)
    return query_hvp.astype(jnp.bfloat16), key_hvp.astype(jnp.bfloat16), value_hvp.astype(jnp.bfloat16), kappa


def split_heads(tensor):
    batch_count = tensor.shape[0]
    length = tensor.shape[1]
    shaped = tensor.reshape(batch_count, length, -1, HEAD_DIM)
    return jnp.transpose(shaped, (0, 2, 1, 3)).reshape(-1, length, HEAD_DIM)


def join_heads(tensor, batch_count):
    length = tensor.shape[1]
    shaped = tensor.reshape(batch_count, -1, length, HEAD_DIM)
    return jnp.transpose(shaped, (0, 2, 1, 3)).reshape(batch_count, length, -1)


def reference(queries, key_rows, value_rows, query_tangent, key_tangent, out_adjoint):
    batch_count = queries.shape[0]
    items = tuple(split_heads(tensor) for tensor in (queries, key_rows, value_rows, query_tangent, key_tangent, out_adjoint))
    query_hvp, key_hvp, value_hvp, kappa = lax.map(head_terms, items)
    curvature = kappa.reshape(batch_count, -1)
    return join_heads(query_hvp, batch_count), join_heads(key_hvp, batch_count), join_heads(value_hvp, batch_count), curvature
```

```python
import functools
import math

import jax
import jax.numpy as jnp
from jax import lax
from jax.experimental import pallas as pl
from jax.experimental.pallas import tpu as pltpu
from jax.sharding import PartitionSpec as P

HEAD_DIM = 128
MESH = pl.DeviceIdType.MESH
F32 = jnp.float32
BF16 = jnp.bfloat16
KEYS = (0, 1, 2)
QUERIES = (3, 4, 5)


def mm(left, right, dims):
    return lax.dot_general(left, right, (dims, ((), ())), preferred_element_type=F32)


def kernel(
    n,
    m,
    local_heads,
    q_in,
    k_in,
    v_in,
    tq_in,
    tk_in,
    g_in,
    q_out,
    k_out,
    v_out,
    curv_out,
    qq,
    kk,
    gg,
    vv,
    hk_acc,
    hv_acc,
    q_staged,
    k_staged,
    v_staged,
    q_low,
    k_low,
    v_low,
    stat_out,
    stat_in,
    mine,
    board,
    x_send,
    x_recv,
    z_send,
    z_recv,
    stat_send,
    stat_recv,
    out_send,
    out_recv,
    low_recv,
    board_send,
    board_recv,
    reach,
):
    D = HEAD_DIM
    me = lax.axis_index("seq")
    dp = lax.axis_index("dp")
    tokens = q_in.shape[1]
    batches = q_in.shape[0]
    quarter = n // 4
    block = quarter * tokens
    factor = D ** (-0.5)
    level = me // quarter
    ring = me % quarter
    place = dp * n + me

    barrier = pltpu.get_barrier_semaphore()

    def hail(sem, seq, row):
        pl.semaphore_signal(sem, inc=1, device_id=(seq, row), device_id_type=MESH)

    def level_mate(step):
        return level * quarter + (ring + step) % quarter

    def column_mate(step):
        return (me + step * quarter) % n

    def greet_level(step, carry):
        hail(barrier, level_mate(step), dp)
        return carry

    def greet_rows(step, carry):
        hail(barrier, me, (dp + step) % m)
        return carry

    for step in range(1, 4):
        hail(barrier, column_mate(step), dp)
    lax.fori_loop(1, quarter, greet_level, 0)
    lax.fori_loop(1, m, greet_rows, 0)
    pl.semaphore_wait(barrier, quarter - 1 + 3 + m - 1)

    tensors = (
        (k_in, kk, 0),
        (tk_in, kk, D),
        (v_in, vv, 0),
        (q_in, qq, D),
        (tq_in, qq, 0),
        (g_in, gg, 0),
    )

    def columns(pair):
        return pl.ds(pl.multiple_of((pair % local_heads) * D, D), D)

    def rows_of(group, index, count=1):
        return slice((group * 4 + index) * block, (group * 4 + index + count) * block)

    def program(here):
        x_waited = set()
        z_waited = set()
        started = set()
        sent = {"z": 0, "stat": 0, "out": 0}
        kappas = {}

        def spread(group, number):
            source, buf, column = tensors[number]
            base = (group * 4 + here) * block
            at = pl.multiple_of(base + ring * tokens, tokens)
            dst = buf.at[pl.ds(at, tokens), column : column + D]
            sem = x_recv.at[group * 6 + number]

            def src(pair):
                return source.at[pair // local_heads, :, columns(pair)]

            def send(step, carry):
                spot = (ring + step) % quarter
                pltpu.make_async_remote_copy(
                    src_ref=src(group * quarter + spot),
                    dst_ref=dst,
                    send_sem=x_send,
                    recv_sem=sem,
                    device_id=(here * quarter + spot, dp),
                    device_id_type=MESH,
                ).start()
                return carry

            pltpu.make_async_copy(src(group * quarter + ring), dst, sem).start()
            lax.fori_loop(1, quarter, send, 0)

        def x_wait(group, number):
            if (group, number) in x_waited:
                return
            x_waited.add((group, number))
            _, buf, column = tensors[number]
            whole = buf.at[rows_of(group, here), column : column + D]
            pltpu.make_async_copy(whole, whole, x_recv.at[group * 6 + number]).wait()

        def relay(group, side, there):
            for number in side:
                x_wait(group, number)
                _, buf, column = tensors[number]
                part = buf.at[rows_of(group, here), column : column + D]
                pltpu.make_async_remote_copy(
                    src_ref=part,
                    dst_ref=part,
                    send_sem=z_send,
                    recv_sem=z_recv.at[(group * 4 + here) * 2 + side[0] // 3],
                    device_id=(there * quarter + ring, dp),
                    device_id_type=MESH,
                ).start()
                sent["z"] += 1

        def need(group, index, side):
            if index == here:
                for number in side:
                    x_wait(group, number)
            elif (group, index, side[0]) not in z_waited:
                z_waited.add((group, index, side[0]))
                whole = vv.at[: 3 * block, :]
                sem = z_recv.at[(group * 4 + index) * 2 + side[0] // 3]
                pltpu.make_async_copy(whole, whole, sem).wait()

        def first(group, index, low, high):
            need(group, index, QUERIES)
            for key in range(low, high):
                need(group, key, KEYS)
            both = qq[rows_of(group, index), :]
            adj = gg[rows_of(group, index), :]
            keys = rows_of(group, low, high - low)
            both_keys = kk[keys, :]
            size = (high - low) * block
            scores = mm(both_keys[:, :D], both[:, D:], ((1,), (1,)))
            if high == index + 1:
                key = lax.broadcasted_iota(jnp.int32, (size, block), 0) + low * block
                row = lax.broadcasted_iota(jnp.int32, (size, block), 1) + index * block
                scores = jnp.where(row >= key, scores, -jnp.inf)
            top = jnp.max(scores, axis=0, keepdims=True)
            weights = jnp.exp2((scores - top) * (factor * math.log2(math.e)))
            tangent = factor * mm(both_keys, both, ((1,), (1,)))
            gprobs = mm(vv[keys, :], adj, ((1,), (1,)))
            moved = weights * tangent
            stats = (
                top,
                jnp.sum(weights, axis=0, keepdims=True),
                jnp.sum(moved, axis=0, keepdims=True),
                jnp.sum(weights * gprobs, axis=0, keepdims=True),
                jnp.sum(moved * gprobs, axis=0, keepdims=True),
            )
            return (weights, tangent, gprobs), stats

        def tell(group, index, stats, there):
            slot = group * 4 + index
            stat_out[slot] = jnp.concatenate(stats + stats[:3], axis=0)
            pltpu.make_async_remote_copy(
                src_ref=stat_out.at[slot],
                dst_ref=stat_in.at[slot],
                send_sem=stat_send,
                recv_sem=stat_recv.at[slot],
                device_id=(there * quarter + ring, dp),
                device_id_type=MESH,
            ).start()
            sent["stat"] += 1

        def merged(group, index, stats):
            slot = group * 4 + index
            pltpu.make_async_copy(stat_in.at[slot], stat_in.at[slot], stat_recv.at[slot]).wait()
            other = stat_in[slot]
            top = jnp.maximum(stats[0], other[0:1, :])
            power = factor * math.log2(math.e)
            ours = jnp.exp2((stats[0] - top) * power)
            theirs = jnp.exp2((other[0:1, :] - top) * power)
            sums = [ours * stats[k] + theirs * other[k : k + 1, :] for k in range(1, 5)]
            return ours, sums

        def second(group, index, low, high, arrays, scale, sums):
            weights, tangent, gprobs = arrays
            over = 1.0 / sums[0]
            mean = sums[1] * over
            delta = sums[2] * over
            tdelta = sums[3] * over - mean * delta
            probs = weights * (over if scale is None else scale * over)
            tprobs = probs * (tangent - mean)
            centered = gprobs - delta
            tprob_low = tprobs.astype(BF16)
            gscore_low = (probs * centered).astype(BF16)
            second_low = (tprobs * centered - probs * tdelta).astype(BF16)
            both = qq[rows_of(group, index), :]
            adj = gg[rows_of(group, index), :]
            both_keys = kk[rows_of(group, low, high - low), :]
            hv = mm(tprob_low, adj, ((1,), (0,)))
            hk = factor * (
                mm(second_low, both[:, D:], ((1,), (0,)))
                + mm(gscore_low, both[:, :D], ((1,), (0,)))
            )
            hq = factor * (
                mm(second_low, both_keys[:, :D], ((0,), (0,)))
                + mm(gscore_low, both_keys[:, D:], ((0,), (0,)))
            )
            for key in range(low, high):
                area = rows_of(group, key)
                part = slice((key - low) * block, (key - low + 1) * block)
                if (group, key) in started:
                    hk_acc[area, :] += hk[part, :]
                    hv_acc[area, :] += hv[part, :]
                else:
                    started.add((group, key))
                    hk_acc[area, :] = hk[part, :]
                    hv_acc[area, :] = hv[part, :]
            owe(group, jnp.sum(both[:, :D].astype(F32) * hq, axis=0, keepdims=True))
            q_staged[rows_of(group, index), :] = hq.astype(BF16)
            ship(group, index, ((q_staged, q_out, q_low, 0),))

        def owe(group, value):
            kappas[group] = kappas[group] + value if group in kappas else value

        def ship(group, index, results):
            pair = group * quarter + ring
            batch = pair // local_heads
            cols = columns(pair)
            base = (group * 4 + index) * block
            home = index == here

            def give(step, carry):
                spot = (ring + step) % quarter
                at = pl.multiple_of(base + spot * tokens, tokens)
                for staged, out, far, number in results:
                    pltpu.make_async_remote_copy(
                        src_ref=staged.at[pl.ds(at, tokens), :],
                        dst_ref=(out if home else far).at[batch, :, cols],
                        send_sem=out_send,
                        recv_sem=(out_recv if home else low_recv).at[number],
                        device_id=(index * quarter + spot, dp),
                        device_id_type=MESH,
                    ).start()
                return carry

            if home:
                at = pl.multiple_of(base + ring * tokens, tokens)
                for staged, out, _, number in results:
                    pltpu.make_async_copy(
                        staged.at[pl.ds(at, tokens), :], out.at[batch, :, cols], out_recv.at[number]
                    ).start()
            lax.fori_loop(1 if home else 0, quarter, give, 0)
            sent["out"] += (quarter - (1 if home else 0)) * len(results)

        def finish(group, index):
            area = rows_of(group, index)
            hk = hk_acc[area, :]
            k_staged[area, :] = hk.astype(BF16)
            v_staged[area, :] = hv_acc[area, :].astype(BF16)
            ship(group, index, ((k_staged, k_out, k_low, 1), (v_staged, v_out, v_low, 2)))
            owe(group, jnp.sum(kk[area, D:].astype(F32) * hk, axis=0, keepdims=True))

        def whole(group, index, low, high):
            arrays, stats = first(group, index, low, high)
            second(group, index, low, high, arrays, None, stats[1:])

        def early(group, index, low, high, there):
            arrays, stats = first(group, index, low, high)
            tell(group, index, stats, there)
            return arrays, stats

        def later(group, index, low, high, held):
            arrays, stats = held
            ours, sums = merged(group, index, stats)
            second(group, index, low, high, arrays, ours, sums)

        def both_ways(group, index, low, high, there):
            later(group, index, low, high, early(group, index, low, high, there))

        def spread_all(order):
            for group, side in order:
                for number in side:
                    spread(group, number)

        def meet():
            pl.semaphore_wait(reach.at[0], 3)
            lax.fori_loop(
                1, m, lambda step, carry: (hail(reach.at[1], me, (dp + step) % m), carry)[1], 0
            )

        K, Q = KEYS, QUERIES
        orders = (
            ((0, K), (2, K), (1, K), (3, K), (0, Q), (2, Q), (1, Q), (3, Q)),
            ((0, K), (0, Q), (1, K), (1, Q), (2, Q), (2, K), (3, Q), (3, K)),
            ((2, Q), (2, K), (3, Q), (3, K), (0, K), (0, Q), (1, K), (1, Q)),
            ((2, Q), (0, Q), (0, K), (2, K), (3, Q), (1, Q), (1, K), (3, K)),
        )
        spread_all(orders[here])
        for step in range(1, 4):
            hail(reach.at[0], column_mate(step), dp)

        if here == 0:
            relay(0, K, 2)
            relay(2, K, 1)
            relay(1, K, 2)
            relay(3, K, 1)
            meet()
            for near, far in ((0, 2), (1, 3)):
                both_ways(near, 1, 0, 1, 1)
                whole(near, 0, 0, 1)
                finish(near, 0)
                whole(far, 0, 0, 1)
                finish(far, 0)
        elif here == 1:
            relay(0, K, 2)
            relay(0, Q, 0)
            relay(1, K, 2)
            relay(1, Q, 0)
            meet()
            held = [early(group, 1, 1, 2, 0) for group in (0, 1)]
            for near, far in ((0, 2), (1, 3)):
                both_ways(far, 2, 0, 2, 2)
                both_ways(far, 3, 0, 2, 3)
                whole(far, 1, 0, 2)
                finish(far, 0)
                finish(far, 1)
                later(near, 1, 1, 2, held[near])
                finish(near, 1)
        elif here == 2:
            relay(2, Q, 1)
            relay(2, K, 3)
            relay(3, Q, 1)
            relay(3, K, 3)
            meet()
            held = [early(group, 2, 2, 3, 1) for group in (2, 3)]
            for near, far in ((0, 2), (1, 3)):
                both_ways(near, 3, 0, 3, 3)
                whole(near, 2, 0, 3)
                finish(near, 0)
                finish(near, 1)
                finish(near, 2)
                later(far, 2, 2, 3, held[near])
                finish(far, 2)
        else:
            relay(2, Q, 1)
            relay(0, Q, 2)
            held = {0: early(0, 3, 3, 4, 2)}
            relay(3, Q, 1)
            relay(1, Q, 2)
            meet()
            held[2] = early(2, 3, 2, 4, 1)
            held[1] = early(1, 3, 3, 4, 2)
            held[3] = early(3, 3, 2, 4, 1)
            for near, far in ((0, 2), (1, 3)):
                later(far, 3, 2, 4, held[far])
                finish(far, 2)
                finish(far, 3)
                later(near, 3, 3, 4, held[near])
                finish(near, 3)

        shape = mine.shape
        total = jnp.zeros(shape, F32)
        row = lax.broadcasted_iota(jnp.int32, shape, 0)
        col = lax.broadcasted_iota(jnp.int32, shape, 1)
        for group in range(4):
            pair = group * quarter + ring
            at_row = row == pair // local_heads
            at_col = col == dp * local_heads + pair % local_heads
            kappa = jnp.sum(kappas[group], keepdims=True)
            total += jnp.where(jnp.logical_and(at_row, at_col), kappa, 0.0)
        mine[...] = total

        pl.semaphore_wait(reach.at[1], m - 1)

        def post(step, carry):
            other = (place + step) % (n * m)
            pltpu.make_async_remote_copy(
                src_ref=mine,
                dst_ref=board.at[place],
                send_sem=board_send,
                recv_sem=board_recv,
                device_id=(other % n, other // n),
                device_id_type=MESH,
            ).start()
            return carry

        pltpu.make_async_copy(mine, board.at[place], board_recv).start()
        lax.fori_loop(1, n * m, post, 0)

        def drain(count, sem):
            part = qq.at[: count // 2, :]
            pltpu.make_async_copy(part, part, sem).wait()

        drain(24 * (quarter - 1) * tokens, x_send)
        drain(sent["z"] * block, z_send)
        stats_sent = stat_out.at[: sent["stat"]]
        pltpu.make_async_copy(stats_sent, stats_sent, stat_send).wait()
        drain(sent["out"] * tokens, out_send)

        middle = batches // 2
        near_half, far_half, full = slice(0, middle), slice(middle, batches), slice(0, batches)
        spans = ((None, full), (near_half, near_half), (far_half, far_half), (full, None))[here]
        targets = ((q_out, q_low), (k_out, k_low), (v_out, v_low))
        for number, span in enumerate((spans[0], spans[1], spans[1])):
            out, far = targets[number]
            pltpu.make_async_copy(out, out, out_recv.at[number]).wait()
            if span is not None:
                extra = far.at[span]
                pltpu.make_async_copy(extra, extra, low_recv.at[number]).wait()
                out[span] = (out[span].astype(F32) + far[span].astype(F32)).astype(BF16)

    for here in range(4):
        pl.when(level == here)(functools.partial(program, here))

    sent = board.at[: n * m - 1]
    pltpu.make_async_copy(sent, sent, board_send).wait()
    pltpu.make_async_copy(board, board, board_recv).wait()
    total = jnp.sum(board[...], axis=0)
    curv_out[...] = total[: curv_out.shape[0], : curv_out.shape[1]]


def local(n, m, queries, key_rows, value_rows, query_tangent, key_tangent, out_adjoint):
    batch, tokens, width = queries.shape
    local_heads = width // HEAD_DIM
    block = n // 4 * tokens
    rows = 16 * block
    heads = local_heads * m
    board_shape = (-(-batch // 8) * 8, -(-heads // 128) * 128)
    result = jax.ShapeDtypeStruct(queries.shape, BF16)
    D = HEAD_DIM
    return pl.pallas_call(
        functools.partial(kernel, n, m, local_heads),
        out_shape=(result, result, result, jax.ShapeDtypeStruct((batch, heads), F32)),
        in_specs=[pl.BlockSpec(memory_space=pl.ANY)] * 6,
        out_specs=(pl.BlockSpec(memory_space=pltpu.VMEM),) * 4,
        scratch_shapes=[
            pltpu.VMEM((rows, 2 * D), BF16),
            pltpu.VMEM((rows, 2 * D), BF16),
            pltpu.VMEM((rows, D), BF16),
            pltpu.VMEM((rows, D), BF16),
            pltpu.VMEM((rows, D), F32),
            pltpu.VMEM((rows, D), F32),
            pltpu.VMEM((rows, D), BF16),
            pltpu.VMEM((rows, D), BF16),
            pltpu.VMEM((rows, D), BF16),
            pltpu.VMEM(queries.shape, BF16),
            pltpu.VMEM(queries.shape, BF16),
            pltpu.VMEM(queries.shape, BF16),
            pltpu.VMEM((16, 8, block), F32),
            pltpu.VMEM((16, 8, block), F32),
            pltpu.VMEM(board_shape, F32),
            pltpu.VMEM((n * m,) + board_shape, F32),
            pltpu.SemaphoreType.DMA,
            pltpu.SemaphoreType.DMA((24,)),
            pltpu.SemaphoreType.DMA,
            pltpu.SemaphoreType.DMA((32,)),
            pltpu.SemaphoreType.DMA,
            pltpu.SemaphoreType.DMA((16,)),
            pltpu.SemaphoreType.DMA,
            pltpu.SemaphoreType.DMA((3,)),
            pltpu.SemaphoreType.DMA((3,)),
            pltpu.SemaphoreType.DMA,
            pltpu.SemaphoreType.DMA,
            pltpu.SemaphoreType.REGULAR((2,)),
        ],
        compiler_params=pltpu.CompilerParams(
            collective_id=0, has_side_effects=True, vmem_limit_bytes=56 * 1024 * 1024
        ),
    )(queries, key_rows, value_rows, query_tangent, key_tangent, out_adjoint)


def solution(mesh):
    split = P(None, "seq", "dp")
    return jax.shard_map(
        functools.partial(local, mesh.shape["seq"], mesh.shape["dp"]),
        mesh=mesh,
        in_specs=(split,) * 6,
        out_specs=(split, split, split, P()),
        check_vma=False,
    )
```

```python
import functools
import math

import jax
import jax.numpy as jnp
from jax import lax
from jax.experimental import pallas as pl
from jax.experimental.pallas import tpu as pltpu
from jax.sharding import PartitionSpec as P

HEAD_DIM = 128
MESH = pl.DeviceIdType.MESH
F32 = jnp.float32
BF16 = jnp.bfloat16
KEYS = (0, 1, 2)
QUERIES = (3, 4, 5)


def mm(left, right, dims):
    return lax.dot_general(left, right, (dims, ((), ())), preferred_element_type=F32)


def kernel(
    n,
    m,
    local_heads,
    q_in,
    k_in,
    v_in,
    tq_in,
    tk_in,
    g_in,
    q_out,
    k_out,
    v_out,
    q_low,
    k_low,
    v_low,
    curv_out,
    qq,
    kk,
    gg,
    vv,
    hk_acc,
    hv_acc,
    q_staged,
    k_staged,
    v_staged,
    stat_out,
    stat_in,
    mine,
    by_level,
    by_ring,
    by_row,
    x_send,
    x_recv,
    z_send,
    z_recv,
    stat_send,
    stat_recv,
    out_send,
    out_recv,
    low_recv,
    board_send,
    board_recv,
    reach,
):
    D = HEAD_DIM
    me = lax.axis_index("seq")
    dp = lax.axis_index("dp")
    tokens = q_in.shape[1]
    batches = q_in.shape[0]
    quarter = n // 4
    block = quarter * tokens
    factor = D ** (-0.5)
    level = me // quarter
    ring = me % quarter

    barrier = pltpu.get_barrier_semaphore()

    def hail(sem, seq, row):
        pl.semaphore_signal(sem, inc=1, device_id=(seq, row), device_id_type=MESH)

    def level_mate(step):
        return level * quarter + (ring + step) % quarter

    def column_mate(step):
        return (me + step * quarter) % n

    def greet_level(step, carry):
        hail(barrier, level_mate(step), dp)
        return carry

    def greet_rows(step, carry):
        hail(barrier, me, (dp + step) % m)
        return carry

    for step in range(1, 4):
        hail(barrier, column_mate(step), dp)
    lax.fori_loop(1, quarter, greet_level, 0)
    lax.fori_loop(1, m, greet_rows, 0)
    pl.semaphore_wait(barrier, quarter - 1 + 3 + m - 1)

    tensors = (
        (k_in, kk, 0),
        (tk_in, kk, D),
        (v_in, vv, 0),
        (q_in, qq, D),
        (tq_in, qq, 0),
        (g_in, gg, 0),
    )

    def columns(pair):
        return pl.ds(pl.multiple_of((pair % local_heads) * D, D), D)

    def rows_of(group, index, count=1):
        return slice((group * 4 + index) * block, (group * 4 + index + count) * block)

    def program(here):
        x_waited = set()
        z_waited = set()
        started = set()
        sent = {"z": 0, "stat": 0, "out": 0}
        kappas = {}

        def spread(group, number):
            source, buf, column = tensors[number]
            base = (group * 4 + here) * block
            at = pl.multiple_of(base + ring * tokens, tokens)
            dst = buf.at[pl.ds(at, tokens), column : column + D]
            sem = x_recv.at[group * 6 + number]

            def src(pair):
                return source.at[pair // local_heads, :, columns(pair)]

            def send(step, carry):
                spot = (ring + step) % quarter
                pltpu.make_async_remote_copy(
                    src_ref=src(group * quarter + spot),
                    dst_ref=dst,
                    send_sem=x_send,
                    recv_sem=sem,
                    device_id=(here * quarter + spot, dp),
                    device_id_type=MESH,
                ).start()
                return carry

            pltpu.make_async_copy(src(group * quarter + ring), dst, sem).start()
            lax.fori_loop(1, quarter, send, 0)

        def x_wait(group, number):
            if (group, number) in x_waited:
                return
            x_waited.add((group, number))
            _, buf, column = tensors[number]
            whole = buf.at[rows_of(group, here), column : column + D]
            pltpu.make_async_copy(whole, whole, x_recv.at[group * 6 + number]).wait()

        def relay(group, side, there):
            for number in side:
                x_wait(group, number)
                _, buf, column = tensors[number]
                part = buf.at[rows_of(group, here), column : column + D]
                pltpu.make_async_remote_copy(
                    src_ref=part,
                    dst_ref=part,
                    send_sem=z_send,
                    recv_sem=z_recv.at[(group * 4 + here) * 2 + side[0] // 3],
                    device_id=(there * quarter + ring, dp),
                    device_id_type=MESH,
                ).start()
                sent["z"] += 1

        def need(group, index, side):
            if index == here:
                for number in side:
                    x_wait(group, number)
            elif (group, index, side[0]) not in z_waited:
                z_waited.add((group, index, side[0]))
                whole = vv.at[: 3 * block, :]
                sem = z_recv.at[(group * 4 + index) * 2 + side[0] // 3]
                pltpu.make_async_copy(whole, whole, sem).wait()

        def first(group, index, low, high):
            need(group, index, QUERIES)
            for key in range(low, high):
                need(group, key, KEYS)
            both = qq[rows_of(group, index), :]
            adj = gg[rows_of(group, index), :]
            keys = rows_of(group, low, high - low)
            both_keys = kk[keys, :]
            size = (high - low) * block
            scores = mm(both_keys[:, :D], both[:, D:], ((1,), (1,)))
            if high == index + 1:
                key = lax.broadcasted_iota(jnp.int32, (size, block), 0) + low * block
                row = lax.broadcasted_iota(jnp.int32, (size, block), 1) + index * block
                scores = jnp.where(row >= key, scores, -jnp.inf)
            top = jnp.max(scores, axis=0, keepdims=True)
            weights = jnp.exp2((scores - top) * (factor * math.log2(math.e)))
            tangent = factor * mm(both_keys, both, ((1,), (1,)))
            gprobs = mm(vv[keys, :], adj, ((1,), (1,)))
            moved = weights * tangent
            stats = (
                top,
                jnp.sum(weights, axis=0, keepdims=True),
                jnp.sum(moved, axis=0, keepdims=True),
                jnp.sum(weights * gprobs, axis=0, keepdims=True),
                jnp.sum(moved * gprobs, axis=0, keepdims=True),
            )
            return (weights, tangent, gprobs), stats

        def tell(group, index, stats, there):
            slot = group * 4 + index
            stat_out[slot] = jnp.concatenate(stats + stats[:3], axis=0)
            pltpu.make_async_remote_copy(
                src_ref=stat_out.at[slot],
                dst_ref=stat_in.at[slot],
                send_sem=stat_send,
                recv_sem=stat_recv.at[slot],
                device_id=(there * quarter + ring, dp),
                device_id_type=MESH,
            ).start()
            sent["stat"] += 1

        def merged(group, index, stats):
            slot = group * 4 + index
            pltpu.make_async_copy(stat_in.at[slot], stat_in.at[slot], stat_recv.at[slot]).wait()
            other = stat_in[slot]
            top = jnp.maximum(stats[0], other[0:1, :])
            power = factor * math.log2(math.e)
            ours = jnp.exp2((stats[0] - top) * power)
            theirs = jnp.exp2((other[0:1, :] - top) * power)
            sums = [ours * stats[k] + theirs * other[k : k + 1, :] for k in range(1, 5)]
            return ours, sums

        def second(group, index, low, high, arrays, scale, sums):
            weights, tangent, gprobs = arrays
            over = 1.0 / sums[0]
            mean = sums[1] * over
            delta = sums[2] * over
            tdelta = sums[3] * over - mean * delta
            probs = weights * (over if scale is None else scale * over)
            tprobs = probs * (tangent - mean)
            centered = gprobs - delta
            tprob_low = tprobs.astype(BF16)
            gscore_low = (probs * centered).astype(BF16)
            second_low = (tprobs * centered - probs * tdelta).astype(BF16)
            both = qq[rows_of(group, index), :]
            adj = gg[rows_of(group, index), :]
            both_keys = kk[rows_of(group, low, high - low), :]
            hv = mm(tprob_low, adj, ((1,), (0,)))
            hk = factor * (
                mm(second_low, both[:, D:], ((1,), (0,)))
                + mm(gscore_low, both[:, :D], ((1,), (0,)))
            )
            hq = factor * (
                mm(second_low, both_keys[:, :D], ((0,), (0,)))
                + mm(gscore_low, both_keys[:, D:], ((0,), (0,)))
            )
            for key in range(low, high):
                area = rows_of(group, key)
                part = slice((key - low) * block, (key - low + 1) * block)
                if (group, key) in started:
                    hk_acc[area, :] += hk[part, :]
                    hv_acc[area, :] += hv[part, :]
                else:
                    started.add((group, key))
                    hk_acc[area, :] = hk[part, :]
                    hv_acc[area, :] = hv[part, :]
            owe(group, jnp.sum(both[:, :D].astype(F32) * hq, axis=0, keepdims=True))
            q_staged[rows_of(group, index), :] = hq.astype(BF16)
            ship(group, index, ((q_staged, q_out, q_low, 0),))

        def owe(group, value):
            kappas[group] = kappas[group] + value if group in kappas else value

        def ship(group, index, results):
            pair = group * quarter + ring
            batch = pair // local_heads
            cols = columns(pair)
            base = (group * 4 + index) * block
            home = index == here

            def give(step, carry):
                spot = (ring + step) % quarter
                at = pl.multiple_of(base + spot * tokens, tokens)
                for staged, out, far, number in results:
                    pltpu.make_async_remote_copy(
                        src_ref=staged.at[pl.ds(at, tokens), :],
                        dst_ref=(out if home else far).at[batch, :, cols],
                        send_sem=out_send,
                        recv_sem=(out_recv if home else low_recv).at[number],
                        device_id=(index * quarter + spot, dp),
                        device_id_type=MESH,
                    ).start()
                return carry

            if home:
                at = pl.multiple_of(base + ring * tokens, tokens)
                for staged, out, _, number in results:
                    pltpu.make_async_copy(
                        staged.at[pl.ds(at, tokens), :], out.at[batch, :, cols], out_recv.at[number]
                    ).start()
            lax.fori_loop(1 if home else 0, quarter, give, 0)
            sent["out"] += (quarter - (1 if home else 0)) * len(results)

        def finish(group, index):
            area = rows_of(group, index)
            hk = hk_acc[area, :]
            k_staged[area, :] = hk.astype(BF16)
            v_staged[area, :] = hv_acc[area, :].astype(BF16)
            ship(group, index, ((k_staged, k_out, k_low, 1), (v_staged, v_out, v_low, 2)))
            owe(group, jnp.sum(kk[area, D:].astype(F32) * hk, axis=0, keepdims=True))

        def whole(group, index, low, high):
            arrays, stats = first(group, index, low, high)
            second(group, index, low, high, arrays, None, stats[1:])

        def early(group, index, low, high, there):
            arrays, stats = first(group, index, low, high)
            tell(group, index, stats, there)
            return arrays, stats

        def later(group, index, low, high, held):
            arrays, stats = held
            ours, sums = merged(group, index, stats)
            second(group, index, low, high, arrays, ours, sums)

        def both_ways(group, index, low, high, there):
            later(group, index, low, high, early(group, index, low, high, there))

        def spread_all(order):
            for group, side in order:
                for number in side:
                    spread(group, number)

        def meet():
            pl.semaphore_wait(reach, 3)

        K, Q = KEYS, QUERIES
        orders = (
            ((0, K), (2, K), (1, K), (3, K), (0, Q), (2, Q), (1, Q), (3, Q)),
            ((0, K), (0, Q), (1, K), (1, Q), (2, Q), (2, K), (3, Q), (3, K)),
            ((2, Q), (2, K), (3, Q), (3, K), (0, K), (0, Q), (1, K), (1, Q)),
            ((2, Q), (0, Q), (0, K), (2, K), (3, Q), (1, Q), (1, K), (3, K)),
        )
        spread_all(orders[here])
        for step in range(1, 4):
            hail(reach, column_mate(step), dp)

        if here == 0:
            relay(0, K, 2)
            relay(2, K, 1)
            relay(1, K, 2)
            relay(3, K, 1)
            meet()
            for near, far in ((0, 2), (1, 3)):
                both_ways(near, 1, 0, 1, 1)
                whole(near, 0, 0, 1)
                finish(near, 0)
                whole(far, 0, 0, 1)
                finish(far, 0)
        elif here == 1:
            relay(0, K, 2)
            relay(0, Q, 0)
            relay(1, K, 2)
            relay(1, Q, 0)
            meet()
            held = [early(group, 1, 1, 2, 0) for group in (0, 1)]
            for near, far in ((0, 2), (1, 3)):
                both_ways(far, 2, 0, 2, 2)
                both_ways(far, 3, 0, 2, 3)
                whole(far, 1, 0, 2)
                finish(far, 0)
                finish(far, 1)
                later(near, 1, 1, 2, held[near])
                finish(near, 1)
        elif here == 2:
            relay(2, Q, 1)
            relay(2, K, 3)
            relay(3, Q, 1)
            relay(3, K, 3)
            meet()
            held = [early(group, 2, 2, 3, 1) for group in (2, 3)]
            for near, far in ((0, 2), (1, 3)):
                both_ways(near, 3, 0, 3, 3)
                whole(near, 2, 0, 3)
                finish(near, 0)
                finish(near, 1)
                finish(near, 2)
                later(far, 2, 2, 3, held[near])
                finish(far, 2)
        else:
            relay(2, Q, 1)
            relay(0, Q, 2)
            held = {0: early(0, 3, 3, 4, 2)}
            relay(3, Q, 1)
            relay(1, Q, 2)
            meet()
            held[2] = early(2, 3, 2, 4, 1)
            held[1] = early(1, 3, 3, 4, 2)
            held[3] = early(3, 3, 2, 4, 1)
            for near, far in ((0, 2), (1, 3)):
                later(far, 3, 2, 4, held[far])
                finish(far, 2)
                finish(far, 3)
                later(near, 3, 3, 4, held[near])
                finish(near, 3)

        shape = mine.shape
        total = jnp.zeros(shape, F32)
        row = lax.broadcasted_iota(jnp.int32, shape, 0)
        col = lax.broadcasted_iota(jnp.int32, shape, 1)
        for group in range(4):
            pair = group * quarter + ring
            at_row = row == pair // local_heads
            at_col = col == dp * local_heads + pair % local_heads
            kappa = jnp.sum(kappas[group], keepdims=True)
            total += jnp.where(jnp.logical_and(at_row, at_col), kappa, 0.0)
        mine[...] = total

        def post(dst, sem, seq, row):
            pltpu.make_async_remote_copy(
                src_ref=mine,
                dst_ref=dst,
                send_sem=board_send,
                recv_sem=board_recv.at[sem],
                device_id=(seq, row),
                device_id_type=MESH,
            ).start()

        def gather(buf, own, count, sem):
            arrivals = buf.at[:count]
            pltpu.make_async_copy(arrivals, arrivals, board_recv.at[sem]).wait()
            buf[own] = mine[...]
            return jnp.sum(buf[...], axis=0)

        def gone(count):
            part = by_ring.at[:count]
            pltpu.make_async_copy(part, part, board_send).wait()

        if here < 3:
            post(by_level.at[here], 0, 3 * quarter + ring, dp)
            gone(1)
        else:
            mine[...] = gather(by_level, 3, 3, 0)

            def post_ring(step, carry):
                post(by_ring.at[ring], 1, level_mate(step), dp)
                return carry

            def post_row(step, carry):
                post(by_row.at[dp], 2, me, (dp + step) % m)
                return carry

            lax.fori_loop(1, quarter, post_ring, 0)
            gone(quarter - 1)
            mine[...] = gather(by_ring, ring, quarter - 1, 1)
            lax.fori_loop(1, m, post_row, 0)
            gone(m - 1)
            mine[...] = gather(by_row, dp, m - 1, 2)
            curv_out[...] = mine[...]
            for there in range(3):
                post(curv_out, 3, there * quarter + ring, dp)
            gone(3)

        def drain(count, sem):
            part = qq.at[: count // 2, :]
            pltpu.make_async_copy(part, part, sem).wait()

        drain(24 * (quarter - 1) * tokens, x_send)
        drain(sent["z"] * block, z_send)
        stats_sent = stat_out.at[: sent["stat"]]
        pltpu.make_async_copy(stats_sent, stats_sent, stat_send).wait()
        drain(sent["out"] * tokens, out_send)

        low_spans = spans_of(here, batches)
        arrivals = ((q_out, q_low), (k_out, k_low), (v_out, v_low))
        for number, (out, far) in enumerate(arrivals):
            pltpu.make_async_copy(out, out, out_recv.at[number]).wait()
            if low_spans[number] is not None:
                extra = far.at[low_spans[number]]
                pltpu.make_async_copy(extra, extra, low_recv.at[number]).wait()
        if here < 3:
            pltpu.make_async_copy(curv_out, curv_out, board_recv.at[3]).wait()

    for here in range(4):
        pl.when(level == here)(functools.partial(program, here))


def spans_of(here, batches):
    middle = batches // 2
    near, far, every = slice(0, middle), slice(middle, batches), slice(0, batches)
    keys, queries = (every, near, far, None)[here], (None, near, far, every)[here]
    return queries, keys, keys


def merge_kernel(n, *refs):
    homes, lows, curv_in = refs[0:3], refs[3:6], refs[6]
    outs, curv_out = refs[7:10], refs[10]
    home_bufs, low_bufs, curv_buf, curv_small = refs[11:14], refs[14:17], refs[17], refs[18]
    in_sems, low_sems, out_sems = refs[19:22]
    level = lax.axis_index("seq") // (n // 4)
    batches = homes[0].shape[0]
    loads = [pltpu.make_async_copy(homes[k], home_bufs[k], in_sems.at[k]) for k in range(3)]
    loads.append(pltpu.make_async_copy(curv_in, curv_buf, in_sems.at[3]))
    stores = [pltpu.make_async_copy(home_bufs[k], outs[k], out_sems.at[k]) for k in range(3)]
    stores.append(pltpu.make_async_copy(curv_small, curv_out, out_sems.at[3]))

    def extra(here, number):
        span = spans_of(here, batches)[number]
        return span, None if span is None else pltpu.make_async_copy(
            lows[number].at[span], low_bufs[number].at[span], low_sems.at[number]
        )

    def fetch(here):
        for number in range(3):
            span, copy = extra(here, number)
            if span is not None:
                copy.start()

    def add(here):
        for number in range(3):
            loads[number].wait()
            span, copy = extra(here, number)
            if span is not None:
                copy.wait()
                total = home_bufs[number][span].astype(F32) + low_bufs[number][span].astype(F32)
                home_bufs[number][span] = total.astype(BF16)
            stores[number].start()

    for copy in loads:
        copy.start()
    for here in range(4):
        pl.when(level == here)(functools.partial(fetch, here))
    loads[3].wait()
    curv_small[...] = curv_buf[: curv_small.shape[0], : curv_small.shape[1]]
    stores[3].start()
    for here in range(4):
        pl.when(level == here)(functools.partial(add, here))
    for copy in stores:
        copy.wait()


def local(n, m, queries, key_rows, value_rows, query_tangent, key_tangent, out_adjoint):
    batch, tokens, width = queries.shape
    local_heads = width // HEAD_DIM
    block = n // 4 * tokens
    rows = 16 * block
    heads = local_heads * m
    board_shape = (-(-batch // 8) * 8, -(-heads // 128) * 128)
    result = jax.ShapeDtypeStruct(queries.shape, BF16)
    D = HEAD_DIM
    anywhere = pl.BlockSpec(memory_space=pl.ANY)
    *parts, curvature = pl.pallas_call(
        functools.partial(kernel, n, m, local_heads),
        out_shape=(result,) * 6 + (jax.ShapeDtypeStruct(board_shape, F32),),
        in_specs=[anywhere] * 6,
        out_specs=(anywhere,) * 6 + (pl.BlockSpec(memory_space=pltpu.VMEM),),
        scratch_shapes=[
            pltpu.VMEM((rows, 2 * D), BF16),
            pltpu.VMEM((rows, 2 * D), BF16),
            pltpu.VMEM((rows, D), BF16),
            pltpu.VMEM((rows, D), BF16),
            pltpu.VMEM((rows, D), F32),
            pltpu.VMEM((rows, D), F32),
            pltpu.VMEM((rows, D), BF16),
            pltpu.VMEM((rows, D), BF16),
            pltpu.VMEM((rows, D), BF16),
            pltpu.VMEM((16, 8, block), F32),
            pltpu.VMEM((16, 8, block), F32),
            pltpu.VMEM(board_shape, F32),
            pltpu.VMEM((4,) + board_shape, F32),
            pltpu.VMEM((n // 4,) + board_shape, F32),
            pltpu.VMEM((m,) + board_shape, F32),
            pltpu.SemaphoreType.DMA,
            pltpu.SemaphoreType.DMA((24,)),
            pltpu.SemaphoreType.DMA,
            pltpu.SemaphoreType.DMA((32,)),
            pltpu.SemaphoreType.DMA,
            pltpu.SemaphoreType.DMA((16,)),
            pltpu.SemaphoreType.DMA,
            pltpu.SemaphoreType.DMA((3,)),
            pltpu.SemaphoreType.DMA((3,)),
            pltpu.SemaphoreType.DMA,
            pltpu.SemaphoreType.DMA((4,)),
            pltpu.SemaphoreType.REGULAR,
        ],
        compiler_params=pltpu.CompilerParams(
            collective_id=0, has_side_effects=True, vmem_limit_bytes=56 * 1024 * 1024
        ),
    )(queries, key_rows, value_rows, query_tangent, key_tangent, out_adjoint)

    return pl.pallas_call(
        functools.partial(merge_kernel, n),
        out_shape=(result, result, result, jax.ShapeDtypeStruct((batch, heads), F32)),
        in_specs=[anywhere] * 7,
        out_specs=(anywhere,) * 4,
        scratch_shapes=[pltpu.VMEM(queries.shape, BF16)] * 6
        + [
            pltpu.VMEM(board_shape, F32),
            pltpu.VMEM((batch, heads), F32),
            pltpu.SemaphoreType.DMA((4,)),
            pltpu.SemaphoreType.DMA((3,)),
            pltpu.SemaphoreType.DMA((4,)),
        ],
    )(*parts, curvature)


def solution(mesh):
    split = P(None, "seq", "dp")
    return jax.shard_map(
        functools.partial(local, mesh.shape["seq"], mesh.shape["dp"]),
        mesh=mesh,
        in_specs=(split,) * 6,
        out_specs=(split, split, split, P()),
        check_vma=False,
    )
```

```python
import functools
import math

import jax
import jax.numpy as jnp
from jax import lax
from jax.experimental import pallas as pl
from jax.experimental.pallas import tpu as pltpu
from jax.sharding import PartitionSpec as P

HEAD_DIM = 128
MESH = pl.DeviceIdType.MESH
F32 = jnp.float32
BF16 = jnp.bfloat16
KEYS = (0, 1, 2)
QUERIES = (3, 4, 5)


def mm(left, right, dims):
    return lax.dot_general(left, right, (dims, ((), ())), preferred_element_type=F32)


def kernel(
    n,
    m,
    local_heads,
    q_in,
    k_in,
    v_in,
    tq_in,
    tk_in,
    g_in,
    q_out,
    k_out,
    v_out,
    q_low,
    k_low,
    v_low,
    curv_out,
    qq,
    kk,
    gg,
    vv,
    hk_acc,
    hv_acc,
    q_staged,
    k_staged,
    v_staged,
    stat_out,
    stat_in,
    mine,
    board,
    x_send,
    x_recv,
    z_send,
    z_recv,
    stat_send,
    stat_recv,
    out_send,
    out_recv,
    low_recv,
    board_send,
    board_recv,
    reach,
):
    D = HEAD_DIM
    me = lax.axis_index("seq")
    dp = lax.axis_index("dp")
    tokens = q_in.shape[1]
    batches = q_in.shape[0]
    quarter = n // 4
    block = quarter * tokens
    factor = D ** (-0.5)
    level = me // quarter
    ring = me % quarter
    place = dp * n + me

    barrier = pltpu.get_barrier_semaphore()

    def hail(sem, seq, row):
        pl.semaphore_signal(sem, inc=1, device_id=(seq, row), device_id_type=MESH)

    def level_mate(step):
        return level * quarter + (ring + step) % quarter

    def greet_level(step, carry):
        hail(barrier, level_mate(step), dp)
        return carry

    def greet_rows(step, carry):
        hail(barrier, me, (dp + step) % m)
        return carry

    def greet_mates(step, carry):
        hail(reach.at[0], me, (dp + step) % m)
        return carry

    lax.fori_loop(1, quarter, greet_level, 0)
    lax.fori_loop(1, m, greet_rows, 0)
    pl.semaphore_wait(barrier, quarter - 1 + m - 1 + (level + 3) // 4)
    pl.when(level < 3)(lambda: hail(barrier, me + quarter, dp))

    tensors = (
        (k_in, kk, 0),
        (tk_in, kk, D),
        (v_in, vv, 0),
        (q_in, qq, D),
        (tq_in, qq, 0),
        (g_in, gg, 0),
    )

    def columns(pair):
        return pl.ds(pl.multiple_of((pair % local_heads) * D, D), D)

    def rows_of(group, index, count=1):
        return slice((group * 4 + index) * block, (group * 4 + index + count) * block)

    def program(here):
        x_waited = set()
        z_waited = set()
        started = set()
        entered = set()
        sent = {"z": 0, "stat": 0, "out": 0}
        kappas = {}

        def spread(group, number):
            source, buf, column = tensors[number]
            base = (group * 4 + here) * block
            at = pl.multiple_of(base + ring * tokens, tokens)
            dst = buf.at[pl.ds(at, tokens), column : column + D]
            sem = x_recv.at[group * 6 + number]

            def src(pair):
                return source.at[pair // local_heads, :, columns(pair)]

            def send(step, carry):
                spot = (ring + step) % quarter
                pltpu.make_async_remote_copy(
                    src_ref=src(group * quarter + spot),
                    dst_ref=dst,
                    send_sem=x_send,
                    recv_sem=sem,
                    device_id=(here * quarter + spot, dp),
                    device_id_type=MESH,
                ).start()
                return carry

            pltpu.make_async_copy(src(group * quarter + ring), dst, sem).start()
            lax.fori_loop(1, quarter, send, 0)

        def x_wait(group, number):
            if (group, number) in x_waited:
                return
            x_waited.add((group, number))
            _, buf, column = tensors[number]
            whole = buf.at[rows_of(group, here), column : column + D]
            pltpu.make_async_copy(whole, whole, x_recv.at[group * 6 + number]).wait()

        def relay(group, side, there):
            known(there)
            for number in side:
                x_wait(group, number)
                _, buf, column = tensors[number]
                part = buf.at[rows_of(group, here), column : column + D]
                pltpu.make_async_remote_copy(
                    src_ref=part,
                    dst_ref=part,
                    send_sem=z_send,
                    recv_sem=z_recv.at[(group * 4 + here) * 2 + side[0] // 3],
                    device_id=(there * quarter + ring, dp),
                    device_id_type=MESH,
                ).start()
                sent["z"] += 1

        def need(group, index, side):
            if index == here:
                for number in side:
                    x_wait(group, number)
            elif (group, index, side[0]) not in z_waited:
                z_waited.add((group, index, side[0]))
                whole = vv.at[: 3 * block, :]
                sem = z_recv.at[(group * 4 + index) * 2 + side[0] // 3]
                pltpu.make_async_copy(whole, whole, sem).wait()

        def first(group, index, low, high):
            need(group, index, QUERIES)
            for key in range(low, high):
                need(group, key, KEYS)
            both = qq[rows_of(group, index), :]
            adj = gg[rows_of(group, index), :]
            keys = rows_of(group, low, high - low)
            both_keys = kk[keys, :]
            size = (high - low) * block
            scores = mm(both_keys[:, :D], both[:, D:], ((1,), (1,)))
            if high == index + 1:
                key = lax.broadcasted_iota(jnp.int32, (size, block), 0) + low * block
                row = lax.broadcasted_iota(jnp.int32, (size, block), 1) + index * block
                scores = jnp.where(row >= key, scores, -jnp.inf)
            top = jnp.max(scores, axis=0, keepdims=True)
            weights = jnp.exp2((scores - top) * (factor * math.log2(math.e)))
            tangent = factor * mm(both_keys, both, ((1,), (1,)))
            gprobs = mm(vv[keys, :], adj, ((1,), (1,)))
            moved = weights * tangent
            stats = (
                top,
                jnp.sum(weights, axis=0, keepdims=True),
                jnp.sum(moved, axis=0, keepdims=True),
                jnp.sum(weights * gprobs, axis=0, keepdims=True),
                jnp.sum(moved * gprobs, axis=0, keepdims=True),
            )
            return (weights, tangent, gprobs), stats

        def tell(group, index, stats, there):
            known(there)
            slot = group * 4 + index
            stat_out[slot] = jnp.concatenate(stats + stats[:3], axis=0)
            pltpu.make_async_remote_copy(
                src_ref=stat_out.at[slot],
                dst_ref=stat_in.at[slot],
                send_sem=stat_send,
                recv_sem=stat_recv.at[slot],
                device_id=(there * quarter + ring, dp),
                device_id_type=MESH,
            ).start()
            sent["stat"] += 1

        def merged(group, index, stats):
            slot = group * 4 + index
            pltpu.make_async_copy(stat_in.at[slot], stat_in.at[slot], stat_recv.at[slot]).wait()
            other = stat_in[slot]
            top = jnp.maximum(stats[0], other[0:1, :])
            power = factor * math.log2(math.e)
            ours = jnp.exp2((stats[0] - top) * power)
            theirs = jnp.exp2((other[0:1, :] - top) * power)
            sums = [ours * stats[k] + theirs * other[k : k + 1, :] for k in range(1, 5)]
            return ours, sums

        def second(group, index, low, high, arrays, scale, sums, now=True):
            weights, tangent, gprobs = arrays
            over = 1.0 / sums[0]
            mean = sums[1] * over
            delta = sums[2] * over
            tdelta = sums[3] * over - mean * delta
            probs = weights * (over if scale is None else scale * over)
            tprobs = probs * (tangent - mean)
            centered = gprobs - delta
            tprob_low = tprobs.astype(BF16)
            gscore_low = (probs * centered).astype(BF16)
            second_low = (tprobs * centered - probs * tdelta).astype(BF16)
            both = qq[rows_of(group, index), :]
            adj = gg[rows_of(group, index), :]
            both_keys = kk[rows_of(group, low, high - low), :]
            hv = mm(tprob_low, adj, ((1,), (0,)))
            hk = factor * (
                mm(second_low, both[:, D:], ((1,), (0,)))
                + mm(gscore_low, both[:, :D], ((1,), (0,)))
            )
            hq = factor * (
                mm(second_low, both_keys[:, :D], ((0,), (0,)))
                + mm(gscore_low, both_keys[:, D:], ((0,), (0,)))
            )
            for key in range(low, high):
                area = rows_of(group, key)
                part = slice((key - low) * block, (key - low + 1) * block)
                if (group, key) in started:
                    hk_acc[area, :] += hk[part, :]
                    hv_acc[area, :] += hv[part, :]
                else:
                    started.add((group, key))
                    hk_acc[area, :] = hk[part, :]
                    hv_acc[area, :] = hv[part, :]
            owe(group, jnp.sum(both[:, :D].astype(F32) * hq, axis=0, keepdims=True))
            q_staged[rows_of(group, index), :] = hq.astype(BF16)
            if now:
                give_queries(group, index)

        def give_queries(group, index):
            ship(group, index, ((q_staged, q_out, q_low, 0),))

        def owe(group, value):
            kappas[group] = kappas[group] + value if group in kappas else value

        def ship(group, index, results):
            pair = group * quarter + ring
            batch = pair // local_heads
            cols = columns(pair)
            base = (group * 4 + index) * block
            home = index == here

            def give(step, carry):
                spot = (ring + step) % quarter
                at = pl.multiple_of(base + spot * tokens, tokens)
                for staged, out, far, number in results:
                    pltpu.make_async_remote_copy(
                        src_ref=staged.at[pl.ds(at, tokens), :],
                        dst_ref=(out if home else far).at[batch, :, cols],
                        send_sem=out_send,
                        recv_sem=(out_recv if home else low_recv).at[number],
                        device_id=(index * quarter + spot, dp),
                        device_id_type=MESH,
                    ).start()
                return carry

            if home:
                at = pl.multiple_of(base + ring * tokens, tokens)
                for staged, out, _, number in results:
                    pltpu.make_async_copy(
                        staged.at[pl.ds(at, tokens), :], out.at[batch, :, cols], out_recv.at[number]
                    ).start()
            lax.fori_loop(1 if home else 0, quarter, give, 0)
            sent["out"] += (quarter - (1 if home else 0)) * len(results)

        def finish(group, index):
            area = rows_of(group, index)
            hk = hk_acc[area, :]
            k_staged[area, :] = hk.astype(BF16)
            v_staged[area, :] = hv_acc[area, :].astype(BF16)
            ship(group, index, ((k_staged, k_out, k_low, 1), (v_staged, v_out, v_low, 2)))
            owe(group, jnp.sum(kk[area, D:].astype(F32) * hk, axis=0, keepdims=True))

        def whole(group, index, low, high):
            arrays, stats = first(group, index, low, high)
            second(group, index, low, high, arrays, None, stats[1:])

        def early(group, index, low, high, there):
            arrays, stats = first(group, index, low, high)
            tell(group, index, stats, there)
            return arrays, stats

        def later(group, index, low, high, held, now=True):
            arrays, stats = held
            ours, sums = merged(group, index, stats)
            second(group, index, low, high, arrays, ours, sums, now)

        def both_ways(group, index, low, high, there, now=True):
            later(group, index, low, high, early(group, index, low, high, there), now)

        def spread_all(*order):
            for group, side in order:
                for number in side:
                    spread(group, number)

        def meet():
            for there in range(here + 1, 4):
                known(there)
            lax.fori_loop(1, m, greet_mates, 0)

        def known(there):
            if there > here and there not in entered:
                entered.add(there)
                pl.semaphore_wait(reach.at[there], 1)

        K, Q = KEYS, QUERIES
        for below in range(here):
            hail(reach.at[here], below * quarter + ring, dp)

        if here == 0:
            spread_all((2, K), (0, K), (3, K))
            relay(2, K, 1)
            relay(0, K, 2)
            spread_all((1, K), (0, Q), (2, Q), (1, Q), (3, Q))
            relay(3, K, 1)
            relay(1, K, 2)
            meet()
            both_ways(0, 1, 0, 1, 1)
            whole(0, 0, 0, 1)
            finish(0, 0)
            for group in (2, 3):
                whole(group, 0, 0, 1)
                finish(group, 0)
            both_ways(1, 1, 0, 1, 1)
            whole(1, 0, 0, 1)
            finish(1, 0)
        elif here == 1:
            spread_all((0, K), (0, Q), (2, Q))
            relay(0, K, 2)
            spread_all((2, K), (1, K))
            relay(0, Q, 0)
            spread_all((1, Q), (3, Q), (3, K))
            held = {0: early(0, 1, 1, 2, 0)}
            meet()
            front = early(2, 2, 0, 2, 2)
            relay(1, K, 2)
            relay(1, Q, 0)
            held[1] = early(1, 1, 1, 2, 0)
            back = early(2, 3, 0, 2, 3)
            later(2, 2, 0, 2, front, False)
            later(2, 3, 0, 2, back, False)
            whole(2, 1, 0, 2)
            finish(2, 0)
            finish(2, 1)
            later(0, 1, 1, 2, held[0])
            finish(0, 1)
            front = early(3, 2, 0, 2, 2)
            back = early(3, 3, 0, 2, 3)
            later(3, 2, 0, 2, front, False)
            later(3, 3, 0, 2, back, False)
            for group in (2, 3):
                give_queries(group, 2)
                give_queries(group, 3)
            whole(3, 1, 0, 2)
            finish(3, 0)
            finish(3, 1)
            later(1, 1, 1, 2, held[1])
            finish(1, 1)
        elif here == 2:
            spread_all((2, Q), (2, K), (0, K))
            relay(2, Q, 1)
            spread_all((0, Q), (3, Q))
            relay(2, K, 3)
            spread_all((3, K), (1, K), (1, Q))
            held = {2: early(2, 2, 2, 3, 1)}
            relay(3, Q, 1)
            relay(3, K, 3)
            meet()
            held[3] = early(3, 2, 2, 3, 1)
            both_ways(0, 3, 0, 3, 3)
            whole(0, 2, 0, 3)
            finish(0, 0)
            finish(0, 1)
            finish(0, 2)
            later(2, 2, 2, 3, held[2])
            finish(2, 2)
            both_ways(1, 3, 0, 3, 3)
            whole(1, 2, 0, 3)
            finish(1, 0)
            finish(1, 1)
            finish(1, 2)
            later(3, 2, 2, 3, held[3])
            finish(3, 2)
        else:
            spread_all((0, Q), (2, Q), (0, K))
            relay(0, Q, 2)
            spread_all((2, K), (1, Q))
            relay(2, Q, 1)
            spread_all((1, K), (3, Q), (3, K))
            held = {0: early(0, 3, 3, 4, 2)}
            meet()
            held[2] = early(2, 3, 2, 4, 1)
            relay(1, Q, 2)
            held[1] = early(1, 3, 3, 4, 2)
            relay(3, Q, 1)
            held[3] = early(3, 3, 2, 4, 1)
            for group in (0, 1):
                later(group, 3, 3, 4, held[group])
                finish(group, 3)
                later(group + 2, 3, 2, 4, held[group + 2])
                finish(group + 2, 2)
                finish(group + 2, 3)

        shape = mine.shape
        total = jnp.zeros(shape, F32)
        row = lax.broadcasted_iota(jnp.int32, shape, 0)
        col = lax.broadcasted_iota(jnp.int32, shape, 1)
        for group in range(4):
            pair = group * quarter + ring
            spot = (pair // local_heads) * (local_heads * m) + dp * local_heads + pair % local_heads
            at_row = row == spot // 128
            at_col = col == spot % 128
            kappa = jnp.sum(kappas[group], keepdims=True)
            total += jnp.where(jnp.logical_and(at_row, at_col), kappa, 0.0)
        mine[...] = total
        pl.semaphore_wait(reach.at[0], m - 1)

        def post(step, carry):
            other = (place + step) % (n * m)
            pltpu.make_async_remote_copy(
                src_ref=mine,
                dst_ref=board.at[place],
                send_sem=board_send,
                recv_sem=board_recv,
                device_id=(other % n, other // n),
                device_id_type=MESH,
            ).start()
            return carry

        pltpu.make_async_copy(mine, board.at[place], board_recv).start()
        lax.fori_loop(1, n * m, post, 0)

        def drain(count, sem):
            part = qq.at[: count // 2, :]
            pltpu.make_async_copy(part, part, sem).wait()

        drain(24 * (quarter - 1) * tokens, x_send)
        drain(sent["z"] * block, z_send)
        stats_sent = stat_out.at[: sent["stat"]]
        pltpu.make_async_copy(stats_sent, stats_sent, stat_send).wait()
        drain(sent["out"] * tokens, out_send)

        low_spans = spans_of(here, batches)
        arrivals = ((q_out, q_low), (k_out, k_low), (v_out, v_low))
        for number, (out, far) in enumerate(arrivals):
            pltpu.make_async_copy(out, out, out_recv.at[number]).wait()
            if low_spans[number] is not None:
                extra = far.at[low_spans[number]]
                pltpu.make_async_copy(extra, extra, low_recv.at[number]).wait()

    for here in range(4):
        pl.when(level == here)(functools.partial(program, here))

    posted = board.at[: n * m - 1]
    pltpu.make_async_copy(posted, posted, board_send).wait()
    pltpu.make_async_copy(board, board, board_recv).wait()
    curv_out[...] = jnp.sum(board[...], axis=0)


def spans_of(here, batches):
    middle = batches // 2
    near, far, every = slice(0, middle), slice(middle, batches), slice(0, batches)
    keys, queries = (every, near, far, None)[here], (None, near, far, every)[here]
    return queries, keys, keys


def merge_kernel(n, *refs):
    homes, lows, curv_in = refs[0:3], refs[3:6], refs[6]
    outs, curv_out = refs[7:10], refs[10]
    home_bufs, low_bufs, curv_buf, curv_small = refs[11:14], refs[14:17], refs[17], refs[18]
    in_sems, low_sems, out_sems = refs[19:22]
    level = lax.axis_index("seq") // (n // 4)
    batches = homes[0].shape[0]
    loads = [pltpu.make_async_copy(homes[k], home_bufs[k], in_sems.at[k]) for k in range(3)]
    loads.append(pltpu.make_async_copy(curv_in, curv_buf, in_sems.at[3]))
    stores = [pltpu.make_async_copy(home_bufs[k], outs[k], out_sems.at[k]) for k in range(3)]
    stores.append(pltpu.make_async_copy(curv_small, curv_out, out_sems.at[3]))

    def extra(here, number):
        span = spans_of(here, batches)[number]
        return span, None if span is None else pltpu.make_async_copy(
            lows[number].at[span], low_bufs[number].at[span], low_sems.at[number]
        )

    def fetch(here):
        for number in range(3):
            span, copy = extra(here, number)
            if span is not None:
                copy.start()

    def add(here):
        for number in range(3):
            loads[number].wait()
            span, copy = extra(here, number)
            if span is not None:
                copy.wait()
                total = home_bufs[number][span].astype(F32) + low_bufs[number][span].astype(F32)
                home_bufs[number][span] = total.astype(BF16)
            stores[number].start()

    for copy in loads:
        copy.start()
    for here in range(4):
        pl.when(level == here)(functools.partial(fetch, here))
    loads[3].wait()
    heads = curv_small.shape[1]
    for batch in range(batches):
        row, lane = batch * heads // 128, batch * heads % 128
        curv_small[batch : batch + 1, :] = curv_buf[row : row + 1, lane : lane + heads]
    stores[3].start()
    for here in range(4):
        pl.when(level == here)(functools.partial(add, here))
    for copy in stores:
        copy.wait()


def local(n, m, queries, key_rows, value_rows, query_tangent, key_tangent, out_adjoint):
    batch, tokens, width = queries.shape
    local_heads = width // HEAD_DIM
    block = n // 4 * tokens
    rows = 16 * block
    heads = local_heads * m
    board_shape = (-(-batch * heads // 128), 128)
    result = jax.ShapeDtypeStruct(queries.shape, BF16)
    D = HEAD_DIM
    anywhere = pl.BlockSpec(memory_space=pl.ANY)
    *parts, curvature = pl.pallas_call(
        functools.partial(kernel, n, m, local_heads),
        out_shape=(result,) * 6 + (jax.ShapeDtypeStruct(board_shape, F32),),
        in_specs=[anywhere] * 6,
        out_specs=(anywhere,) * 6 + (pl.BlockSpec(memory_space=pltpu.VMEM),),
        scratch_shapes=[
            pltpu.VMEM((rows, 2 * D), BF16),
            pltpu.VMEM((rows, 2 * D), BF16),
            pltpu.VMEM((rows, D), BF16),
            pltpu.VMEM((rows, D), BF16),
            pltpu.VMEM((rows, D), F32),
            pltpu.VMEM((rows, D), F32),
            pltpu.VMEM((rows, D), BF16),
            pltpu.VMEM((rows, D), BF16),
            pltpu.VMEM((rows, D), BF16),
            pltpu.VMEM((16, 8, block), F32),
            pltpu.VMEM((16, 8, block), F32),
            pltpu.VMEM(board_shape, F32),
            pltpu.VMEM((n * m,) + board_shape, F32),
            pltpu.SemaphoreType.DMA,
            pltpu.SemaphoreType.DMA((24,)),
            pltpu.SemaphoreType.DMA,
            pltpu.SemaphoreType.DMA((32,)),
            pltpu.SemaphoreType.DMA,
            pltpu.SemaphoreType.DMA((16,)),
            pltpu.SemaphoreType.DMA,
            pltpu.SemaphoreType.DMA((3,)),
            pltpu.SemaphoreType.DMA((3,)),
            pltpu.SemaphoreType.DMA,
            pltpu.SemaphoreType.DMA,
            pltpu.SemaphoreType.REGULAR((4,)),
        ],
        compiler_params=pltpu.CompilerParams(
            collective_id=0, has_side_effects=True, vmem_limit_bytes=56 * 1024 * 1024
        ),
    )(queries, key_rows, value_rows, query_tangent, key_tangent, out_adjoint)

    return pl.pallas_call(
        functools.partial(merge_kernel, n),
        out_shape=(result, result, result, jax.ShapeDtypeStruct((batch, heads), F32)),
        in_specs=[anywhere] * 7,
        out_specs=(anywhere,) * 4,
        scratch_shapes=[pltpu.VMEM(queries.shape, BF16)] * 6
        + [
            pltpu.VMEM(board_shape, F32),
            pltpu.VMEM((batch, heads), F32),
            pltpu.SemaphoreType.DMA((4,)),
            pltpu.SemaphoreType.DMA((3,)),
            pltpu.SemaphoreType.DMA((4,)),
        ],
    )(*parts, curvature)


def solution(mesh):
    split = P(None, "seq", "dp")
    return jax.shard_map(
        functools.partial(local, mesh.shape["seq"], mesh.shape["dp"]),
        mesh=mesh,
        in_specs=(split,) * 6,
        out_specs=(split, split, split, P()),
        check_vma=False,
    )
```

```python
import functools
import math

import jax
import jax.numpy as jnp
from jax import lax
from jax.experimental import pallas as pl
from jax.experimental.pallas import tpu as pltpu
from jax.sharding import PartitionSpec as P

HEAD_DIM = 128
MESH = pl.DeviceIdType.MESH
F32 = jnp.float32
BF16 = jnp.bfloat16
KEYS = (0, 1, 2)
QUERIES = (3, 4, 5)


def mm(left, right, dims):
    return lax.dot_general(left, right, (dims, ((), ())), preferred_element_type=F32)


def kernel(
    n,
    m,
    local_heads,
    q_in,
    k_in,
    v_in,
    tq_in,
    tk_in,
    g_in,
    q_out,
    k_out,
    v_out,
    q_low,
    k_low,
    v_low,
    curv_out,
    qq,
    kk,
    gg,
    vv,
    hk_acc,
    hv_acc,
    q_staged,
    k_staged,
    v_staged,
    stat_out,
    stat_in,
    mine,
    board,
    x_send,
    x_recv,
    z_send,
    z_recv,
    stat_send,
    stat_recv,
    out_send,
    out_recv,
    low_recv,
    board_send,
    board_recv,
    reach,
):
    D = HEAD_DIM
    me = lax.axis_index("seq")
    dp = lax.axis_index("dp")
    tokens = q_in.shape[1]
    batches = q_in.shape[0]
    quarter = n // 4
    block = quarter * tokens
    factor = D ** (-0.5)
    level = me // quarter
    ring = me % quarter
    place = dp * n + me

    barrier = pltpu.get_barrier_semaphore()

    def hail(sem, seq, row):
        pl.semaphore_signal(sem, inc=1, device_id=(seq, row), device_id_type=MESH)

    def level_mate(step):
        return level * quarter + (ring + step) % quarter

    def greet_level(step, carry):
        hail(barrier, level_mate(step), dp)
        return carry

    def greet_rows(step, carry):
        hail(barrier, me, (dp + step) % m)
        return carry

    def greet_mates(step, carry):
        hail(reach.at[0], me, (dp + step) % m)
        return carry

    lax.fori_loop(1, quarter, greet_level, 0)
    lax.fori_loop(1, m, greet_rows, 0)
    pl.semaphore_wait(barrier, quarter - 1 + m - 1 + (level + 3) // 4)
    pl.when(level < 3)(lambda: hail(barrier, me + quarter, dp))

    tensors = (
        (k_in, kk, 0),
        (tk_in, kk, D),
        (v_in, vv, 0),
        (q_in, qq, D),
        (tq_in, qq, 0),
        (g_in, gg, 0),
    )

    def columns(pair):
        return pl.ds(pl.multiple_of((pair % local_heads) * D, D), D)

    def rows_of(group, index, count=1):
        return slice((group * 4 + index) * block, (group * 4 + index + count) * block)

    def program(here):
        x_waited = set()
        z_waited = set()
        started = set()
        entered = set()
        sent = {"z": 0, "stat": 0, "out": 0}
        kappas = {}

        def spread(group, number):
            source, buf, column = tensors[number]
            base = (group * 4 + here) * block
            at = pl.multiple_of(base + ring * tokens, tokens)
            dst = buf.at[pl.ds(at, tokens), column : column + D]
            sem = x_recv.at[group * 6 + number]

            def src(pair):
                return source.at[pair // local_heads, :, columns(pair)]

            def send(step, carry):
                spot = (ring + step) % quarter
                pltpu.make_async_remote_copy(
                    src_ref=src(group * quarter + spot),
                    dst_ref=dst,
                    send_sem=x_send,
                    recv_sem=sem,
                    device_id=(here * quarter + spot, dp),
                    device_id_type=MESH,
                ).start()
                return carry

            pltpu.make_async_copy(src(group * quarter + ring), dst, sem).start()
            lax.fori_loop(1, quarter, send, 0)

        def x_wait(group, number):
            if (group, number) in x_waited:
                return
            x_waited.add((group, number))
            _, buf, column = tensors[number]
            whole = buf.at[rows_of(group, here), column : column + D]
            pltpu.make_async_copy(whole, whole, x_recv.at[group * 6 + number]).wait()

        def relay(group, side, there):
            known(there)
            for number in side:
                x_wait(group, number)
                _, buf, column = tensors[number]
                part = buf.at[rows_of(group, here), column : column + D]
                pltpu.make_async_remote_copy(
                    src_ref=part,
                    dst_ref=part,
                    send_sem=z_send,
                    recv_sem=z_recv.at[(group * 4 + here) * 2 + side[0] // 3],
                    device_id=(there * quarter + ring, dp),
                    device_id_type=MESH,
                ).start()
                sent["z"] += 1

        def need(group, index, side):
            if index == here:
                for number in side:
                    x_wait(group, number)
            elif (group, index, side[0]) not in z_waited:
                z_waited.add((group, index, side[0]))
                whole = vv.at[: 3 * block, :]
                sem = z_recv.at[(group * 4 + index) * 2 + side[0] // 3]
                pltpu.make_async_copy(whole, whole, sem).wait()

        def first(group, index, low, high):
            need(group, index, QUERIES)
            for key in range(low, high):
                need(group, key, KEYS)
            both = qq[rows_of(group, index), :]
            adj = gg[rows_of(group, index), :]
            keys = rows_of(group, low, high - low)
            both_keys = kk[keys, :]
            size = (high - low) * block
            scores = mm(both_keys[:, :D], both[:, D:], ((1,), (1,)))
            if high == index + 1:
                key = lax.broadcasted_iota(jnp.int32, (size, block), 0) + low * block
                row = lax.broadcasted_iota(jnp.int32, (size, block), 1) + index * block
                scores = jnp.where(row >= key, scores, -jnp.inf)
            top = jnp.max(scores, axis=0, keepdims=True)
            weights = jnp.exp2((scores - top) * (factor * math.log2(math.e)))
            tangent = factor * mm(both_keys, both, ((1,), (1,)))
            gprobs = mm(vv[keys, :], adj, ((1,), (1,)))
            moved = weights * tangent
            stats = (
                top,
                jnp.sum(weights, axis=0, keepdims=True),
                jnp.sum(moved, axis=0, keepdims=True),
                jnp.sum(weights * gprobs, axis=0, keepdims=True),
                jnp.sum(moved * gprobs, axis=0, keepdims=True),
            )
            return (weights, tangent, gprobs), stats

        def tell(group, index, stats, there):
            known(there)
            slot = group * 4 + index
            stat_out[slot] = jnp.concatenate(stats + stats[:3], axis=0)
            pltpu.make_async_remote_copy(
                src_ref=stat_out.at[slot],
                dst_ref=stat_in.at[slot],
                send_sem=stat_send,
                recv_sem=stat_recv.at[slot],
                device_id=(there * quarter + ring, dp),
                device_id_type=MESH,
            ).start()
            sent["stat"] += 1

        def merged(group, index, stats):
            slot = group * 4 + index
            pltpu.make_async_copy(stat_in.at[slot], stat_in.at[slot], stat_recv.at[slot]).wait()
            other = stat_in[slot]
            top = jnp.maximum(stats[0], other[0:1, :])
            power = factor * math.log2(math.e)
            ours = jnp.exp2((stats[0] - top) * power)
            theirs = jnp.exp2((other[0:1, :] - top) * power)
            sums = [ours * stats[k] + theirs * other[k : k + 1, :] for k in range(1, 5)]
            return ours, sums

        def second(group, index, low, high, arrays, scale, sums, now=True):
            weights, tangent, gprobs = arrays
            over = 1.0 / sums[0]
            mean = sums[1] * over
            delta = sums[2] * over
            tdelta = sums[3] * over - mean * delta
            probs = weights * (over if scale is None else scale * over)
            tprobs = probs * (tangent - mean)
            centered = gprobs - delta
            tprob_low = tprobs.astype(BF16)
            gscore_low = (probs * centered).astype(BF16)
            second_low = (tprobs * centered - probs * tdelta).astype(BF16)
            both = qq[rows_of(group, index), :]
            adj = gg[rows_of(group, index), :]
            both_keys = kk[rows_of(group, low, high - low), :]
            hv = mm(tprob_low, adj, ((1,), (0,)))
            hk = factor * (
                mm(second_low, both[:, D:], ((1,), (0,)))
                + mm(gscore_low, both[:, :D], ((1,), (0,)))
            )
            hq = factor * (
                mm(second_low, both_keys[:, :D], ((0,), (0,)))
                + mm(gscore_low, both_keys[:, D:], ((0,), (0,)))
            )
            for key in range(low, high):
                area = rows_of(group, key)
                part = slice((key - low) * block, (key - low + 1) * block)
                if (group, key) in started:
                    hk_acc[area, :] += hk[part, :]
                    hv_acc[area, :] += hv[part, :]
                else:
                    started.add((group, key))
                    hk_acc[area, :] = hk[part, :]
                    hv_acc[area, :] = hv[part, :]
            owe(group, jnp.sum(both[:, :D].astype(F32) * hq, axis=0, keepdims=True))
            q_staged[rows_of(group, index), :] = hq.astype(BF16)
            if now:
                give_queries(group, index)

        def give_queries(group, index):
            ship(group, index, ((q_staged, q_out, q_low, 0),))

        def owe(group, value):
            kappas[group] = kappas[group] + value if group in kappas else value

        def ship(group, index, results):
            pair = group * quarter + ring
            batch = pair // local_heads
            cols = columns(pair)
            base = (group * 4 + index) * block
            home = index == here

            def give(step, carry):
                spot = (ring + step) % quarter
                at = pl.multiple_of(base + spot * tokens, tokens)
                for staged, out, far, number in results:
                    pltpu.make_async_remote_copy(
                        src_ref=staged.at[pl.ds(at, tokens), :],
                        dst_ref=(out if home else far).at[batch, :, cols],
                        send_sem=out_send,
                        recv_sem=(out_recv if home else low_recv).at[number],
                        device_id=(index * quarter + spot, dp),
                        device_id_type=MESH,
                    ).start()
                return carry

            if home:
                at = pl.multiple_of(base + ring * tokens, tokens)
                for staged, out, _, number in results:
                    pltpu.make_async_copy(
                        staged.at[pl.ds(at, tokens), :], out.at[batch, :, cols], out_recv.at[number]
                    ).start()
            lax.fori_loop(1 if home else 0, quarter, give, 0)
            sent["out"] += (quarter - (1 if home else 0)) * len(results)

        def finish(group, index):
            area = rows_of(group, index)
            hk = hk_acc[area, :]
            k_staged[area, :] = hk.astype(BF16)
            v_staged[area, :] = hv_acc[area, :].astype(BF16)
            ship(group, index, ((k_staged, k_out, k_low, 1), (v_staged, v_out, v_low, 2)))
            owe(group, jnp.sum(kk[area, D:].astype(F32) * hk, axis=0, keepdims=True))

        def whole(group, index, low, high):
            arrays, stats = first(group, index, low, high)
            second(group, index, low, high, arrays, None, stats[1:])

        def early(group, index, low, high, there):
            arrays, stats = first(group, index, low, high)
            tell(group, index, stats, there)
            return arrays, stats

        def later(group, index, low, high, held, now=True):
            arrays, stats = held
            ours, sums = merged(group, index, stats)
            second(group, index, low, high, arrays, ours, sums, now)

        def both_ways(group, index, low, high, there, now=True):
            later(group, index, low, high, early(group, index, low, high, there), now)

        def spread_all(*order):
            for group, side in order:
                for number in side:
                    spread(group, number)

        def meet():
            for there in range(here + 1, 4):
                known(there)
            lax.fori_loop(1, m, greet_mates, 0)

        def known(there):
            if there > here and there not in entered:
                entered.add(there)
                pl.semaphore_wait(reach.at[there], 1)

        K, Q = KEYS, QUERIES
        for below in range(here):
            hail(reach.at[here], below * quarter + ring, dp)

        if here == 0:
            spread_all((2, K), (0, K), (1, K))
            relay(2, K, 1)
            relay(0, K, 2)
            spread_all((3, K), (0, Q), (2, Q), (1, Q), (3, Q))
            relay(1, K, 2)
            relay(3, K, 1)
            meet()
            both_ways(0, 1, 0, 1, 1)
            whole(0, 0, 0, 1)
            finish(0, 0)
            for group in (2, 3):
                whole(group, 0, 0, 1)
                finish(group, 0)
            both_ways(1, 1, 0, 1, 1)
            whole(1, 0, 0, 1)
            finish(1, 0)
        elif here == 1:
            spread_all((0, K), (0, Q), (2, Q))
            relay(0, K, 2)
            spread_all((2, K), (1, K))
            relay(0, Q, 0)
            spread_all((1, Q), (3, Q), (3, K))
            held = {0: early(0, 1, 1, 2, 0)}
            meet()
            front = early(2, 2, 0, 2, 2)
            relay(1, K, 2)
            relay(1, Q, 0)
            held[1] = early(1, 1, 1, 2, 0)
            back = early(2, 3, 0, 2, 3)
            later(2, 2, 0, 2, front, False)
            later(2, 3, 0, 2, back, False)
            whole(2, 1, 0, 2)
            finish(2, 0)
            finish(2, 1)
            later(0, 1, 1, 2, held[0])
            finish(0, 1)
            front = early(3, 2, 0, 2, 2)
            back = early(3, 3, 0, 2, 3)
            later(3, 2, 0, 2, front, False)
            later(3, 3, 0, 2, back, False)
            for group in (2, 3):
                give_queries(group, 2)
                give_queries(group, 3)
            whole(3, 1, 0, 2)
            finish(3, 0)
            finish(3, 1)
            later(1, 1, 1, 2, held[1])
            finish(1, 1)
        elif here == 2:
            spread_all((2, Q), (2, K), (0, K))
            relay(2, Q, 1)
            spread_all((0, Q), (3, Q))
            relay(2, K, 3)
            spread_all((3, K), (1, K), (1, Q))
            held = {2: early(2, 2, 2, 3, 1)}
            relay(3, Q, 1)
            relay(3, K, 3)
            meet()
            held[3] = early(3, 2, 2, 3, 1)
            both_ways(0, 3, 0, 3, 3)
            whole(0, 2, 0, 3)
            finish(0, 0)
            finish(0, 1)
            finish(0, 2)
            later(2, 2, 2, 3, held[2])
            finish(2, 2)
            both_ways(1, 3, 0, 3, 3)
            whole(1, 2, 0, 3)
            finish(1, 0)
            finish(1, 1)
            finish(1, 2)
            later(3, 2, 2, 3, held[3])
            finish(3, 2)
        else:
            spread_all((0, Q), (2, Q), (0, K))
            relay(0, Q, 2)
            spread_all((2, K), (1, Q))
            relay(2, Q, 1)
            spread_all((1, K), (3, Q), (3, K))
            held = {0: early(0, 3, 3, 4, 2)}
            meet()
            held[2] = early(2, 3, 2, 4, 1)
            relay(1, Q, 2)
            held[1] = early(1, 3, 3, 4, 2)
            relay(3, Q, 1)
            held[3] = early(3, 3, 2, 4, 1)
            for group in (0, 1):
                later(group, 3, 3, 4, held[group])
                finish(group, 3)
                later(group + 2, 3, 2, 4, held[group + 2])
                finish(group + 2, 2)
                finish(group + 2, 3)

        shape = mine.shape
        total = jnp.zeros(shape, F32)
        row = lax.broadcasted_iota(jnp.int32, shape, 0)
        col = lax.broadcasted_iota(jnp.int32, shape, 1)
        for group in range(4):
            pair = group * quarter + ring
            spot = (pair // local_heads) * (local_heads * m) + dp * local_heads + pair % local_heads
            at_row = row == spot // 128
            at_col = col == spot % 128
            kappa = jnp.sum(kappas[group], keepdims=True)
            total += jnp.where(jnp.logical_and(at_row, at_col), kappa, 0.0)
        mine[...] = total
        pl.semaphore_wait(reach.at[0], m - 1)

        def post(step, carry):
            other = (place + step) % (n * m)
            pltpu.make_async_remote_copy(
                src_ref=mine,
                dst_ref=board.at[place],
                send_sem=board_send,
                recv_sem=board_recv,
                device_id=(other % n, other // n),
                device_id_type=MESH,
            ).start()
            return carry

        pltpu.make_async_copy(mine, board.at[place], board_recv).start()
        lax.fori_loop(1, n * m, post, 0)

        def drain(count, sem):
            part = qq.at[: count // 2, :]
            pltpu.make_async_copy(part, part, sem).wait()

        drain(24 * (quarter - 1) * tokens, x_send)
        drain(sent["z"] * block, z_send)
        stats_sent = stat_out.at[: sent["stat"]]
        pltpu.make_async_copy(stats_sent, stats_sent, stat_send).wait()
        drain(sent["out"] * tokens, out_send)

        low_spans = spans_of(here, batches)
        arrivals = ((q_out, q_low), (k_out, k_low), (v_out, v_low))
        for number, (out, far) in enumerate(arrivals):
            pltpu.make_async_copy(out, out, out_recv.at[number]).wait()
            if low_spans[number] is not None:
                extra = far.at[low_spans[number]]
                pltpu.make_async_copy(extra, extra, low_recv.at[number]).wait()

    for here in range(4):
        pl.when(level == here)(functools.partial(program, here))

    posted = board.at[: n * m - 1]
    pltpu.make_async_copy(posted, posted, board_send).wait()
    pltpu.make_async_copy(board, board, board_recv).wait()
    curv_out[...] = jnp.sum(board[...], axis=0)


def spans_of(here, batches):
    middle = batches // 2
    near, far, every = slice(0, middle), slice(middle, batches), slice(0, batches)
    keys, queries = (every, near, far, None)[here], (None, near, far, every)[here]
    return queries, keys, keys


def merge_kernel(n, *refs):
    homes, lows, curv_in = refs[0:3], refs[3:6], refs[6]
    outs, curv_out = refs[7:10], refs[10]
    home_bufs, low_bufs, curv_buf, curv_small = refs[11:14], refs[14:17], refs[17], refs[18]
    in_sems, low_sems, out_sems = refs[19:22]
    level = lax.axis_index("seq") // (n // 4)
    batches = homes[0].shape[0]
    loads = [pltpu.make_async_copy(homes[k], home_bufs[k], in_sems.at[k]) for k in range(3)]
    loads.append(pltpu.make_async_copy(curv_in, curv_buf, in_sems.at[3]))
    stores = [pltpu.make_async_copy(home_bufs[k], outs[k], out_sems.at[k]) for k in range(3)]
    stores.append(pltpu.make_async_copy(curv_small, curv_out, out_sems.at[3]))

    def extra(here, number):
        span = spans_of(here, batches)[number]
        return span, None if span is None else pltpu.make_async_copy(
            lows[number].at[span], low_bufs[number].at[span], low_sems.at[number]
        )

    def fetch(here):
        for number in range(3):
            span, copy = extra(here, number)
            if span is not None:
                copy.start()

    def add(here):
        for number in range(3):
            loads[number].wait()
            span, copy = extra(here, number)
            if span is not None:
                copy.wait()
                total = home_bufs[number][span].astype(F32) + low_bufs[number][span].astype(F32)
                home_bufs[number][span] = total.astype(BF16)
            stores[number].start()

    for copy in loads:
        copy.start()
    for here in range(4):
        pl.when(level == here)(functools.partial(fetch, here))
    loads[3].wait()
    heads = curv_small.shape[1]
    for batch in range(batches):
        row, lane = batch * heads // 128, batch * heads % 128
        curv_small[batch : batch + 1, :] = curv_buf[row : row + 1, lane : lane + heads]
    stores[3].start()
    for here in range(4):
        pl.when(level == here)(functools.partial(add, here))
    for copy in stores:
        copy.wait()


def local(n, m, queries, key_rows, value_rows, query_tangent, key_tangent, out_adjoint):
    batch, tokens, width = queries.shape
    local_heads = width // HEAD_DIM
    block = n // 4 * tokens
    rows = 16 * block
    heads = local_heads * m
    board_shape = (-(-batch * heads // 128), 128)
    result = jax.ShapeDtypeStruct(queries.shape, BF16)
    D = HEAD_DIM
    anywhere = pl.BlockSpec(memory_space=pl.ANY)
    *parts, curvature = pl.pallas_call(
        functools.partial(kernel, n, m, local_heads),
        out_shape=(result,) * 6 + (jax.ShapeDtypeStruct(board_shape, F32),),
        in_specs=[anywhere] * 6,
        out_specs=(anywhere,) * 6 + (pl.BlockSpec(memory_space=pltpu.VMEM),),
        scratch_shapes=[
            pltpu.VMEM((rows, 2 * D), BF16),
            pltpu.VMEM((rows, 2 * D), BF16),
            pltpu.VMEM((rows, D), BF16),
            pltpu.VMEM((rows, D), BF16),
            pltpu.VMEM((rows, D), F32),
            pltpu.VMEM((rows, D), F32),
            pltpu.VMEM((rows, D), BF16),
            pltpu.VMEM((rows, D), BF16),
            pltpu.VMEM((rows, D), BF16),
            pltpu.VMEM((16, 8, block), F32),
            pltpu.VMEM((16, 8, block), F32),
            pltpu.VMEM(board_shape, F32),
            pltpu.VMEM((n * m,) + board_shape, F32),
            pltpu.SemaphoreType.DMA,
            pltpu.SemaphoreType.DMA((24,)),
            pltpu.SemaphoreType.DMA,
            pltpu.SemaphoreType.DMA((32,)),
            pltpu.SemaphoreType.DMA,
            pltpu.SemaphoreType.DMA((16,)),
            pltpu.SemaphoreType.DMA,
            pltpu.SemaphoreType.DMA((3,)),
            pltpu.SemaphoreType.DMA((3,)),
            pltpu.SemaphoreType.DMA,
            pltpu.SemaphoreType.DMA,
            pltpu.SemaphoreType.REGULAR((4,)),
        ],
        compiler_params=pltpu.CompilerParams(
            collective_id=0, has_side_effects=True, vmem_limit_bytes=56 * 1024 * 1024
        ),
    )(queries, key_rows, value_rows, query_tangent, key_tangent, out_adjoint)

    return pl.pallas_call(
        functools.partial(merge_kernel, n),
        out_shape=(result, result, result, jax.ShapeDtypeStruct((batch, heads), F32)),
        in_specs=[anywhere] * 7,
        out_specs=(anywhere,) * 4,
        scratch_shapes=[pltpu.VMEM(queries.shape, BF16)] * 6
        + [
            pltpu.VMEM(board_shape, F32),
            pltpu.VMEM((batch, heads), F32),
            pltpu.SemaphoreType.DMA((4,)),
            pltpu.SemaphoreType.DMA((3,)),
            pltpu.SemaphoreType.DMA((4,)),
        ],
    )(*parts, curvature)


def solution(mesh):
    split = P(None, "seq", "dp")
    return jax.shard_map(
        functools.partial(local, mesh.shape["seq"], mesh.shape["dp"]),
        mesh=mesh,
        in_specs=(split,) * 6,
        out_specs=(split, split, split, P()),
        check_vma=False,
    )
```
